32 devices in a mesh: ctx: 8 (over z, core), fsdp: 4 (over y, x).
Axes of the slice: x: 2, y: 2, z: 4, core: 2. Of those that a mesh axis runs over, the one named last changes fastest.
Arguments:
- tokens: bfloat16 [4, 4096, 768], P('fsdp', 'ctx'), may hold values from -6 to 6
- encoder_states: bfloat16 [4, 1500, 768], P('fsdp'), may hold values from -6 to 6
- lengths: int32 [4], P('fsdp'), may hold values from 1024 to 4096, as said below
- cotangent: bfloat16 [4, 4096, 768], P('fsdp', 'ctx'), may hold values from -6 to 6
- first_gain: bfloat16 [768], P('fsdp'), may hold values from 0.5 to 1.5
- first_shift: bfloat16 [768], P('fsdp'), may hold values from -1.5 to 1.5
- query_weight: bfloat16 [768, 768], P('fsdp'), may hold values from -0.21875 to 0.21875
- query_bias: bfloat16 [768], P('fsdp'), may hold values from -1.5 to 1.5
- key_weight: bfloat16 [768, 768], P('fsdp'), may hold values from -0.21875 to 0.21875
- value_weight: bfloat16 [768, 768], P('fsdp'), may hold values from -0.21875 to 0.21875
- value_bias: bfloat16 [768], P('fsdp'), may hold values from -1.5 to 1.5
- self_out_weight: bfloat16 [768, 768], P('fsdp'), may hold values from -3.5 to 3.5
- self_out_bias: bfloat16 [768], P('fsdp'), may hold values from -1.5 to 1.5
- second_gain: bfloat16 [768], P('fsdp'), may hold values from 0.5 to 1.5
- second_shift: bfloat16 [768], P('fsdp'), may hold values from -1.5 to 1.5
- cross_query_weight: bfloat16 [768, 768], P('fsdp'), may hold values from -0.21875 to 0.21875
- cross_query_bias: bfloat16 [768], P('fsdp'), may hold values from -1.5 to 1.5
- cross_key_weight: bfloat16 [768, 768], P('fsdp'), may hold values from -0.21875 to 0.21875
- cross_value_weight: bfloat16 [768, 768], P('fsdp'), may hold values from -0.21875 to 0.21875
- cross_value_bias: bfloat16 [768], P('fsdp'), may hold values from -1.5 to 1.5
- cross_out_weight: bfloat16 [768, 768], P('fsdp'), may hold values from -3.5 to 3.5
- cross_out_bias: bfloat16 [768], P('fsdp'), may hold values from -1.5 to 1.5
- third_gain: bfloat16 [768], P('fsdp'), may hold values from 0.5 to 1.5
- third_shift: bfloat16 [768], P('fsdp'), may hold values from -1.5 to 1.5
- expand_weight: bfloat16 [768, 3072], P('fsdp'), may hold values from -0.21875 to 0.21875
- expand_bias: bfloat16 [3072], P('fsdp'), may hold values from -1.5 to 1.5
- reduce_weight: bfloat16 [3072, 768], P('fsdp'), may hold values from -0.109375 to 0.109375
- reduce_bias: bfloat16 [768], P('fsdp'), may hold values from -2.5 to 2.5
Outputs:
- layer_out: float32 [4, 4096, 768], P('fsdp', 'ctx')
- token_grads: float32 [4, 4096, 768], P('fsdp', 'ctx')
- encoder_grads: float32 [4, 1500, 768], P('fsdp')
- gradient_first_gain: float32 [768], P('fsdp')
- gradient_first_shift: float32 [768], P('fsdp')
- gradient_query_weight: float32 [768, 768], P('fsdp')
- gradient_query_bias: float32 [768], P('fsdp')
- gradient_key_weight: float32 [768, 768], P('fsdp')
- gradient_value_weight: float32 [768, 768], P('fsdp')
- gradient_value_bias: float32 [768], P('fsdp')
- gradient_self_out_weight: float32 [768, 768], P('fsdp')
- gradient_self_out_bias: float32 [768], P('fsdp')
- gradient_second_gain: float32 [768], P('fsdp')
- gradient_second_shift: float32 [768], P('fsdp')
- gradient_cross_query_weight: float32 [768, 768], P('fsdp')
- gradient_cross_query_bias: float32 [768], P('fsdp')
- gradient_cross_key_weight: float32 [768, 768], P('fsdp')
- gradient_cross_value_weight: float32 [768, 768], P('fsdp')
- gradient_cross_value_bias: float32 [768], P('fsdp')
- gradient_cross_out_weight: float32 [768, 768], P('fsdp')
- gradient_cross_out_bias: float32 [768], P('fsdp')
- gradient_third_gain: float32 [768], P('fsdp')
- gradient_third_shift: float32 [768], P('fsdp')
- gradient_expand_weight: float32 [768, 3072], P('fsdp')
- gradient_expand_bias: float32 [3072], P('fsdp')
- gradient_reduce_weight: float32 [3072, 768], P('fsdp')
- gradient_reduce_bias: float32 [768], P('fsdp')
The draws below stay inside these ranges and needn't reach their ends.
Inputs may be any that keep to these rules, and one draw needn't show every extreme that they name: `lengths`: real tokens of each slot fill its first positions; in every draw one slot is full and one holds exactly 1024 real tokens.
All inputs are finite; a program needn't handle non-finite values.
Results may differ from the reference program's by a relative error of at most 0.033.
Values may be sent and summed in bfloat16 or wider, within the bound.
A program may use at most 320 MiB of HBM per device.

```python
import jax
import jax.numpy as jnp
from jax import lax

D = 768
HEADS = 12
HEAD_DIM = 64
FF = 3072
FRAMES = 1500
SLOT_LEN = 4096
MIN_LEN = 1024
SLOTS = 4


def draw_lengths(key, part):
    first_key, second_key = jax.random.split(jax.random.fold_in(key, 11))
    lengths_drawn = jax.random.randint(first_key, (SLOTS,), MIN_LEN, SLOT_LEN + 1, dtype=jnp.int32)
    slot_order = jax.random.permutation(second_key, SLOTS)
    lengths_drawn = lengths_drawn.at[slot_order[0]].set(SLOT_LEN)
    lengths_drawn = lengths_drawn.at[slot_order[1]].set(MIN_LEN)
    return lengths_drawn.astype(jnp.int32)


def levels(stream_key, shape, pieces, least, high):
    def one(position, blocks):
        steps = jax.random.uniform(jax.random.fold_in(jax.random.fold_in(stream_key, 6), position), (blocks,), jnp.float32, least / len(pieces), high / len(pieces))
        return jnp.repeat(jnp.exp(steps), shape[position] // blocks).reshape((-1,) + (1,) * (len(shape) - position - 1))

    factor_of = one(*pieces[0])
    for cut in pieces[1:]:
        factor_of = factor_of * one(*cut)
    return factor_of


def scatter_about(own_key, shape, width, bound, cuts=(), kind=jnp.bfloat16):
    values = jax.random.normal(own_key, shape, jnp.float32) * width
    if len(cuts) > 0:
        values = levels(own_key, shape, cuts, -0.22, 0.18) * values
    return jnp.clip(values, min=-bound, max=bound).astype(kind)


def setup_inputs(seed: int = 0) -> dict:
    seeds = jax.random.split(jax.random.key(seed), 29)
    return {
        "tokens": scatter_about(seeds[0], (SLOTS, SLOT_LEN, D), 1.0, 6.0, ((0, 4), (1, 8))),
        "encoder_states": scatter_about(seeds[1], (SLOTS, FRAMES, D), 1.0, 6.0, ((0, 4),)),
        "lengths": draw_lengths(jax.random.fold_in(seeds[28], 71), 0),
        "cotangent": scatter_about(seeds[3], (SLOTS, SLOT_LEN, D), 1.0, 6.0, ((0, 4), (1, 8))),
        "first_gain": jnp.clip(1.0 + 0.1 * jax.random.normal(seeds[4], (D,), jnp.float32), 0.5, 1.5).astype(jnp.bfloat16),
        "first_shift": scatter_about(seeds[5], (D,), 0.3, 1.5, ((0, 4),)),
        "query_weight": scatter_about(seeds[6], (D, D), D ** -0.5, 0.21875, ((0, 4),)),
        "query_bias": scatter_about(seeds[7], (D,), 0.3, 1.5, ((0, 4),)),
        "key_weight": scatter_about(seeds[8], (D, D), D ** -0.5, 0.21875, ((0, 4),)),
        "value_weight": scatter_about(seeds[9], (D, D), D ** -0.5, 0.21875, ((0, 4),)),
        "value_bias": scatter_about(seeds[10], (D,), 0.3, 1.5, ((0, 4),)),
        "self_out_weight": scatter_about(seeds[11], (D, D), (max(D // 256, 1)) ** -0.5, 3.5, ((0, 4),)),
        "self_out_bias": scatter_about(seeds[12], (D,), 0.3, 1.5, ((0, 4),)),
        "second_gain": jnp.clip(1.0 + 0.1 * jax.random.normal(seeds[13], (D,), jnp.float32), 0.5, 1.5).astype(jnp.bfloat16),
        "second_shift": scatter_about(seeds[14], (D,), 0.3, 1.5, ((0, 4),)),
        "cross_query_weight": scatter_about(seeds[15], (D, D), D ** -0.5, 0.21875, ((0, 4),)),
        "cross_query_bias": scatter_about(seeds[16], (D,), 0.3, 1.5, ((0, 4),)),
        "cross_key_weight": scatter_about(seeds[17], (D, D), D ** -0.5, 0.21875, ((0, 4),)),
        "cross_value_weight": scatter_about(seeds[18], (D, D), D ** -0.5, 0.21875, ((0, 4),)),
        "cross_value_bias": scatter_about(seeds[19], (D,), 0.3, 1.5, ((0, 4),)),
        "cross_out_weight": scatter_about(seeds[20], (D, D), (max(D // 256, 1)) ** -0.5, 3.5, ((0, 4),)),
        "cross_out_bias": scatter_about(seeds[21], (D,), 0.3, 1.5, ((0, 4),)),
        "third_gain": jnp.clip(1.0 + 0.1 * jax.random.normal(seeds[22], (D,), jnp.float32), 0.5, 1.5).astype(jnp.bfloat16),
        "third_shift": scatter_about(seeds[23], (D,), 0.3, 1.5, ((0, 4),)),
        "expand_weight": scatter_about(seeds[24], (D, FF), D ** -0.5, 0.21875, ((0, 4),)),
        "expand_bias": scatter_about(seeds[25], (FF,), 0.3, 1.5, ((0, 4),)),
        "reduce_weight": scatter_about(seeds[26], (FF, D), FF ** -0.5, 0.109375, ((0, 4),)),
        "reduce_bias": scatter_about(seeds[27], (D,), 0.5, 2.5, ((0, 4),)),
    }


eps = 1e-05
masked = -1e+30
highest_precision = lax.Precision.HIGHEST

@jax.custom_vjp
def low(v):
    return lax.optimization_barrier(v.astype(jnp.bfloat16)).astype(jnp.float32)

@jax.custom_vjp
def low_back(v):
    return v

def low_keep(v):
    return (low(v), None)

def low_pass(kept, grad):
    return (grad,)

def back_keep(v):
    return (v, None)

def back_low(kept, grad):
    return (low(grad),)
low.defvjp(low_keep, low_pass)
low_back.defvjp(back_keep, back_low)

def layer_norm(input_rows, norm_gain, norm_shift):
    centre = lax.optimization_barrier(jnp.mean(input_rows, axis=-1, keepdims=True))
    centered = input_rows - centre
    spread = lax.optimization_barrier(jnp.mean(centered * centered, axis=-1, keepdims=True))
    return centered * lax.rsqrt(spread + eps) * norm_gain + norm_shift

def linear(input_rows, weight_matrix):
    return jnp.einsum('...d,df->...f', input_rows, weight_matrix, precision=highest_precision)

def split_heads(input_rows):
    return input_rows.reshape(input_rows.shape[:-1] + (HEADS, HEAD_DIM))

def merge_heads(input_rows):
    return input_rows.reshape(input_rows.shape[:-2] + (HEADS * HEAD_DIM,))

def self_slot(slot_items):
    query_rows, key_rows, value_rows, length = slot_items
    block_rows = min(512, SLOT_LEN)
    score_scale = HEAD_DIM ** (-0.5)
    key_pos = jnp.arange(SLOT_LEN, dtype=jnp.int32)

    def one_block(block_start):
        query_block = lax.dynamic_slice_in_dim(query_rows, block_start, block_rows, 0)
        query_pos = block_start + jnp.arange(block_rows, dtype=jnp.int32)
        allowed = (key_pos[None, None, :] <= query_pos[None, :, None]) & (key_pos[None, None, :] < length)
        scores = jnp.einsum('qhe,khe->hqk', split_heads(query_block), split_heads(key_rows), precision=highest_precision) * score_scale
        scores = jnp.where(allowed, low_back(scores), masked)
        row_top = lax.optimization_barrier(jnp.max(scores, axis=-1, keepdims=True))
        weights = jnp.exp(scores - row_top)
        probability = low(weights / lax.optimization_barrier(jnp.sum(weights, axis=-1, keepdims=True)))
        return merge_heads(jnp.einsum('hqk,khe->qhe', probability, split_heads(value_rows), precision=highest_precision))
    starts = jnp.arange(SLOT_LEN // block_rows, dtype=jnp.int32) * block_rows
    mixed_blocks = lax.map(jax.checkpoint(one_block), starts)
    return mixed_blocks.reshape(SLOT_LEN, HEADS * HEAD_DIM)

def cross_slot(slot_items):
    query_rows, key_rows, value_rows = slot_items
    block_rows = min(512, SLOT_LEN)
    score_scale = HEAD_DIM ** (-0.5)

    def one_block(block_start):
        query_block = lax.dynamic_slice_in_dim(query_rows, block_start, block_rows, 0)
        scores = jnp.einsum('qhe,khe->hqk', split_heads(query_block), split_heads(key_rows), precision=highest_precision) * score_scale
        scores = low_back(scores)
        row_top = lax.optimization_barrier(jnp.max(scores, axis=-1, keepdims=True))
        weights = jnp.exp(scores - row_top)
        probability = low(weights / lax.optimization_barrier(jnp.sum(weights, axis=-1, keepdims=True)))
        return merge_heads(jnp.einsum('hqk,khe->qhe', probability, split_heads(value_rows), precision=highest_precision))
    starts = jnp.arange(SLOT_LEN // block_rows, dtype=jnp.int32) * block_rows
    mixed_blocks = lax.map(jax.checkpoint(one_block), starts)
    return mixed_blocks.reshape(SLOT_LEN, HEADS * HEAD_DIM)

def decoder_layer(residual, encoder, params, lengths, valid_rows):
    first_gain, first_shift, query_weight, query_bias, key_weight, value_weight, value_bias, self_out_weight, self_out_bias, second_gain, second_shift, cross_query_weight, cross_query_bias, cross_key_weight, cross_value_weight, cross_value_bias, cross_out_weight, cross_out_bias, third_gain, third_shift, expand_weight, expand_bias, reduce_weight, reduce_bias = params
    normed = low(layer_norm(residual, first_gain, first_shift))
    query_rows = low_back(low(linear(normed, query_weight) + query_bias))
    key_rows = low_back(low(linear(normed, key_weight)))
    value_rows = low_back(low(linear(normed, value_weight) + value_bias))
    mixed_rows = low_back(low(lax.map(self_slot, (query_rows, key_rows, value_rows, lengths))))
    after_self = residual + low_back(linear(mixed_rows, self_out_weight) + self_out_bias)
    normed = low(layer_norm(after_self, second_gain, second_shift))
    cross_query = low_back(low(linear(normed, cross_query_weight) + cross_query_bias))
    cross_keys = low_back(low(linear(encoder, cross_key_weight)))
    cross_values = low_back(low(linear(encoder, cross_value_weight) + cross_value_bias))
    cross_mixed = low_back(low(lax.map(cross_slot, (cross_query, cross_keys, cross_values))))
    after_cross = after_self + low_back(linear(cross_mixed, cross_out_weight) + cross_out_bias)
    normed = low(layer_norm(after_cross, third_gain, third_shift))
    expanded = low_back(linear(normed, expand_weight) + expand_bias)
    activated = low(jax.nn.gelu(expanded, approximate=False))
    result = after_cross + low_back(linear(activated, reduce_weight) + reduce_bias)
    return result * valid_rows

def reference(tokens, encoder_states, lengths, cotangent, first_gain, first_shift, query_weight, query_bias, key_weight, value_weight, value_bias, self_out_weight, self_out_bias, second_gain, second_shift, cross_query_weight, cross_query_bias, cross_key_weight, cross_value_weight, cross_value_bias, cross_out_weight, cross_out_bias, third_gain, third_shift, expand_weight, expand_bias, reduce_weight, reduce_bias):
    params = tuple((entry.astype(jnp.float32) for entry in (first_gain, first_shift, query_weight, query_bias, key_weight, value_weight, value_bias, self_out_weight, self_out_bias, second_gain, second_shift, cross_query_weight, cross_query_bias, cross_key_weight, cross_value_weight, cross_value_bias, cross_out_weight, cross_out_bias, third_gain, third_shift, expand_weight, expand_bias, reduce_weight, reduce_bias)))
    positions = jnp.arange(SLOT_LEN, dtype=jnp.int32)
    valid_rows = (positions[None, :] < lengths[:, None]).astype(jnp.float32)[:, :, None]

    def forward(residual, encoder, weights):
        return decoder_layer(residual, encoder, weights, lengths, valid_rows)
    result, pullback = jax.vjp(forward, tokens.astype(jnp.float32), encoder_states.astype(jnp.float32), params)
    token_grads, encoder_grads, param_grads = pullback(cotangent.astype(jnp.float32))
    return (result, token_grads, encoder_grads, param_grads[0], param_grads[1], param_grads[2], param_grads[3], param_grads[4], param_grads[5], param_grads[6], param_grads[7], param_grads[8], param_grads[9], param_grads[10], param_grads[11], param_grads[12], param_grads[13], param_grads[14], param_grads[15], param_grads[16], param_grads[17], param_grads[18], param_grads[19], param_grads[20], param_grads[21], param_grads[22], param_grads[23])
```

```python
import functools
import math

import jax
import jax.numpy as jnp
from jax import lax
from jax.experimental import pallas as pl
from jax.experimental.pallas import tpu as pltpu
from jax.sharding import Mesh
from jax.sharding import PartitionSpec as P

HEADS = 12
HEAD_DIM = 64
SCALE = HEAD_DIM ** (-0.5)
EPS = 1e-05
MASKED = -1e30
BF = jnp.bfloat16
F32 = jnp.float32


def cost(flops, nbytes, exps=0):
    return pl.CostEstimate(flops=int(flops), bytes_accessed=int(nbytes), transcendentals=int(exps))


def params(axes):
    return pltpu.CompilerParams(
        dimension_semantics=("arbitrary",) * axes, vmem_limit_bytes=60 * 1024 * 1024
    )


def masked_heads(flat, hg):
    zero = jnp.zeros((HEAD_DIM, flat.shape[1]), flat.dtype)
    out = []
    for h in range(hg):
        rows = [zero] * hg
        rows[h] = flat[h * HEAD_DIM : (h + 1) * HEAD_DIM]
        out.append(jnp.concatenate(rows, axis=0))
    return out


def tile_mask(block_pos, tile_start, shape, length, causal):
    key = tile_start + lax.broadcasted_iota(jnp.int32, shape, 0)
    inside = key < length
    if causal:
        query = block_pos + lax.broadcasted_iota(jnp.int32, shape, 1)
        inside = inside & (key <= query)
    return inside


def tile_bounds(base, qt, kt, length, causal, total):
    if causal:
        full = jnp.minimum(base, length) // kt
        end = (jnp.minimum(base + qt, length) + kt - 1) // kt
        return full, end
    return length // kt, (length + kt - 1) // kt


def fwd_kernel(hg, qt, kt, causal, rows_of, info, q_ref, k_ref, v_ref, o_ref, ob_ref, lse_ref,
               vt, qm, acc, mx, sm):
    block = pl.program_id(1)
    total = k_ref.shape[0]
    width = hg * HEAD_DIM

    @pl.when(block == 0)
    def _():
        vt[...] = v_ref[...].T

    flat = (q_ref[...] * BF(SCALE)).T
    for h, piece in enumerate(masked_heads(flat, hg)):
        qm[h] = piece
    acc[...] = jnp.zeros_like(acc)
    sm[...] = jnp.zeros_like(sm)
    mx[...] = jnp.full_like(mx, MASKED)
    base = rows_of(block, info)
    length = info[0]

    def step(j, masked):
        start = pl.multiple_of(j * kt, kt)
        keys = k_ref[pl.ds(start, kt), :]
        if masked:
            allowed = tile_mask(base, start, (kt, qt), length, causal)
        scores, tops = [], []
        for h in range(hg):
            s = jnp.dot(keys, qm[h], preferred_element_type=F32)
            if masked:
                s = jnp.where(allowed, s, MASKED)
            scores.append(s)
            tops.append(jnp.max(s, axis=0, keepdims=True))
        for h in range(hg):
            old = mx[h : h + 1, :]
            new = jnp.maximum(old, tops[h])
            p = jnp.exp(scores[h] - new)
            fix = jnp.exp(old - new)
            mx[h : h + 1, :] = new
            sm[h : h + 1, :] = sm[h : h + 1, :] * fix + jnp.sum(p, axis=0, keepdims=True)
            here = slice(h * HEAD_DIM, (h + 1) * HEAD_DIM)
            acc[here, :] = acc[here, :] * fix + jnp.dot(
                vt[here, pl.ds(start, kt)], p.astype(BF), preferred_element_type=F32
            )

    if causal:
        full, end = tile_bounds(base, qt, kt, length, causal, total)

        @pl.loop(0, full)
        def _(j):
            step(j, False)

        @pl.loop(full, end)
        def _(j):
            step(j, True)
    else:
        tiles = total // kt
        for j in range(tiles):
            step(j, j == tiles - 1)

    for h in range(hg):
        here = slice(h * HEAD_DIM, (h + 1) * HEAD_DIM)
        acc[here, :] = acc[here, :] / sm[h : h + 1, :]
    out = acc[...].T
    o_ref[...] = out
    ob_ref[...] = out.astype(BF)
    lse_ref[0, 0] = mx[:hg, :] + jnp.log(sm[:hg, :])


def bwd_kernel(hg, qt, kt, causal, rows_of, info, q_ref, do_ref, o_ref, lse_ref, k_ref, v_ref,
               dq_ref, dk_ref, dv_ref, kt_ref, qm, dm, qs, ds_, dk, dv, dqt, dl):
    block = pl.program_id(1)
    total = k_ref.shape[0]

    @pl.when(block == 0)
    def _():
        kt_ref[...] = k_ref[...].T
        dk[...] = jnp.zeros_like(dk)
        dv[...] = jnp.zeros_like(dv)

    q = q_ref[...] * BF(SCALE)
    do = do_ref[...]
    qflat = q.T
    dflat = do.T
    prod = (do.astype(F32) * o_ref[...]).T
    lane = lax.broadcasted_iota(jnp.int32, (qt, hg * HEAD_DIM), 1) // HEAD_DIM
    qpieces = masked_heads(qflat, hg)
    dpieces = masked_heads(dflat, hg)
    for h in range(hg):
        qm[h] = qpieces[h]
        dm[h] = dpieces[h]
        keep = lane == h
        qs[h * qt : (h + 1) * qt, :] = jnp.where(keep, q, jnp.zeros_like(q))
        ds_[h * qt : (h + 1) * qt, :] = jnp.where(keep, do, jnp.zeros_like(do))
        dl[h : h + 1, :] = jnp.sum(prod[h * HEAD_DIM : (h + 1) * HEAD_DIM], axis=0, keepdims=True)
    dqt[...] = jnp.zeros_like(dqt)
    base = rows_of(block, info)
    length = info[0]

    def step(j, masked):
        start = pl.multiple_of(j * kt, kt)
        keys = k_ref[pl.ds(start, kt), :]
        values = v_ref[pl.ds(start, kt), :]
        if masked:
            allowed = tile_mask(base, start, (kt, qt), length, causal)
        ps, gs = [], []
        for h in range(hg):
            s = jnp.dot(keys, qm[h], preferred_element_type=F32)
            p = jnp.exp(s - lse_ref[0, 0, h : h + 1, :])
            if masked:
                p = jnp.where(allowed, p, 0.0)
            dp = jnp.dot(values, dm[h], preferred_element_type=F32)
            g = (p * (dp - dl[h : h + 1, :])).astype(BF)
            ps.append(p.astype(BF))
            gs.append(g)
            here = slice(h * HEAD_DIM, (h + 1) * HEAD_DIM)
            dqt[here, :] += jnp.dot(kt_ref[here, pl.ds(start, kt)], g, preferred_element_type=F32)
        where = pl.ds(start, kt)
        dv[where, :] += jnp.dot(
            jnp.concatenate(ps, axis=1), ds_[...], preferred_element_type=F32
        )
        dk[where, :] += jnp.dot(
            jnp.concatenate(gs, axis=1), qs[...], preferred_element_type=F32
        )

    if causal:
        full, end = tile_bounds(base, qt, kt, length, causal, total)

        @pl.loop(0, full)
        def _(j):
            step(j, False)

        @pl.loop(full, end)
        def _(j):
            step(j, True)
    else:
        tiles = total // kt
        for j in range(tiles):
            step(j, j == tiles - 1)

    dq_ref[...] = (dqt[...] * SCALE).T.astype(BF)

    @pl.when(block == pl.num_programs(1) - 1)
    def _():
        dk_ref[...] = dk[...].astype(BF)
        dv_ref[...] = dv[...].astype(BF)


def flash_fwd(q, k, v, info, hg, qt, kt, causal, blocks, q_index, rows_of, name):
    total, all_width = k.shape
    width = hg * HEAD_DIM
    groups = all_width // width
    rows = blocks * qt
    pairs = rows * total * HEADS * (1 if not causal else 0.5) * groups * hg / HEADS
    return pl.pallas_call(
        functools.partial(fwd_kernel, hg, qt, kt, causal, rows_of),
        grid_spec=pltpu.PrefetchScalarGridSpec(
            num_scalar_prefetch=1,
            grid=(groups, blocks),
            in_specs=[
                pl.BlockSpec((qt, width), lambda g, i, s: (q_index(i, s), g)),
                pl.BlockSpec((total, width), lambda g, i, s: (0, g)),
                pl.BlockSpec((total, width), lambda g, i, s: (0, g)),
            ],
            out_specs=[
                pl.BlockSpec((qt, width), lambda g, i, s: (i, g)),
                pl.BlockSpec((qt, width), lambda g, i, s: (i, g)),
                pl.BlockSpec((1, 1, hg, qt), lambda g, i, s: (g, i, 0, 0)),
            ],
            scratch_shapes=[
                pltpu.VMEM((width, total), BF),
                pltpu.VMEM((hg, width, qt), BF),
                pltpu.VMEM((width, qt), F32),
                pltpu.VMEM((8, qt), F32),
                pltpu.VMEM((8, qt), F32),
            ],
        ),
        out_shape=[
            jax.ShapeDtypeStruct((rows, all_width), F32),
            jax.ShapeDtypeStruct((rows, all_width), BF),
            jax.ShapeDtypeStruct((groups, blocks, hg, qt), F32),
        ],
        compiler_params=params(2),
        cost_estimate=cost(pairs * 4 * 256, rows * all_width * 8 + total * all_width * 4, pairs),
        name=name,
    )(info, q, k, v)


def flash_bwd(q, do, o, lse, k, v, info, hg, qt, kt, causal, blocks, q_index, rows_of, name):
    total, all_width = k.shape
    width = hg * HEAD_DIM
    groups = all_width // width
    rows = blocks * qt
    pairs = rows * total * HEADS * (1 if not causal else 0.5) * groups * hg / HEADS
    return pl.pallas_call(
        functools.partial(bwd_kernel, hg, qt, kt, causal, rows_of),
        grid_spec=pltpu.PrefetchScalarGridSpec(
            num_scalar_prefetch=1,
            grid=(groups, blocks),
            in_specs=[
                pl.BlockSpec((qt, width), lambda g, i, s: (q_index(i, s), g)),
                pl.BlockSpec((qt, width), lambda g, i, s: (i, g)),
                pl.BlockSpec((qt, width), lambda g, i, s: (i, g)),
                pl.BlockSpec((1, 1, hg, qt), lambda g, i, s: (g, i, 0, 0)),
                pl.BlockSpec((total, width), lambda g, i, s: (0, g)),
                pl.BlockSpec((total, width), lambda g, i, s: (0, g)),
            ],
            out_specs=[
                pl.BlockSpec((qt, width), lambda g, i, s: (i, g)),
                pl.BlockSpec((total, width), lambda g, i, s: (0, g)),
                pl.BlockSpec((total, width), lambda g, i, s: (0, g)),
            ],
            scratch_shapes=[
                pltpu.VMEM((width, total), BF),
                pltpu.VMEM((hg, width, qt), BF),
                pltpu.VMEM((hg, width, qt), BF),
                pltpu.VMEM((hg * qt, width), BF),
                pltpu.VMEM((hg * qt, width), BF),
                pltpu.VMEM((total, width), F32),
                pltpu.VMEM((total, width), F32),
                pltpu.VMEM((width, qt), F32),
                pltpu.VMEM((8, qt), F32),
            ],
        ),
        out_shape=[
            jax.ShapeDtypeStruct((rows, all_width), BF),
            jax.ShapeDtypeStruct((total, all_width), BF),
            jax.ShapeDtypeStruct((total, all_width), BF),
        ],
        compiler_params=params(2),
        cost_estimate=cost(pairs * 10 * 256, rows * all_width * 10 + total * all_width * 8, pairs),
        name=name,
    )(info, q, do, o, lse, k, v)


def ln_qkv_kernel(x_ref, w_ref, add_ref, gain_ref, shift_ref, n_ref, q_ref, k_ref, v_ref):
    x = x_ref[...].astype(F32)
    centre = jnp.mean(x, axis=-1, keepdims=True)
    x = x - centre
    spread = jnp.mean(x * x, axis=-1, keepdims=True)
    n = (x * lax.rsqrt(spread + EPS) * gain_ref[...] + shift_ref[...]).astype(BF)
    n_ref[...] = n
    width = q_ref.shape[1]
    y = jnp.dot(n, w_ref[...], preferred_element_type=F32) + add_ref[...]
    y = y.astype(BF)
    q_ref[...] = y[:, :width]
    k_ref[...] = y[:, width : 2 * width]
    v_ref[...] = y[:, 2 * width :]


def ln_qkv(x, w, add, gain, shift, rows):
    total, d = x.shape
    width = w.shape[1] // 3
    whole = lambda a: pl.BlockSpec(a.shape, lambda i: (0, 0))
    return pl.pallas_call(
        ln_qkv_kernel,
        grid=(total // rows,),
        in_specs=[pl.BlockSpec((rows, d), lambda i: (i, 0)), whole(w), whole(add), whole(gain), whole(shift)],
        out_specs=[pl.BlockSpec((rows, d), lambda i: (i, 0))]
        + [pl.BlockSpec((rows, width), lambda i: (i, 0))] * 3,
        out_shape=[jax.ShapeDtypeStruct((total, d), BF)]
        + [jax.ShapeDtypeStruct((total, width), BF)] * 3,
        compiler_params=params(1),
        cost_estimate=cost(2 * total * d * 3 * width, total * d * 4 + total * width * 6),
        name="ln_qkv",
    )(x, w, add, gain, shift)


def ffn_kernel(n_ref, up_ref, we_ref, wr_ref, be_ref, out_ref, dn_ref, dwe_ref, dwr_ref, dbe_ref, nt):
    step = pl.program_id(0)

    @pl.when(step == 0)
    def _():
        nt[...] = n_ref[...].T
        out_ref[...] = jnp.zeros_like(out_ref)
        dn_ref[...] = jnp.zeros_like(dn_ref)

    we = we_ref[...]
    wr = wr_ref[...]
    up = up_ref[...]
    h = jnp.dot(n_ref[...], we, preferred_element_type=F32) + be_ref[...]
    half = 0.5 + 0.5 * lax.erf(h * (2.0**-0.5))
    act = (h * half).astype(BF)
    slope = half + h * jnp.exp(-0.5 * h * h) * ((2.0 * math.pi) ** -0.5)
    out_ref[...] += jnp.dot(act, wr, preferred_element_type=F32)
    da = lax.dot_general(up, wr, (((1,), (1,)), ((), ())), preferred_element_type=F32)
    dh32 = da * slope
    dh = dh32.astype(BF)
    dn_ref[...] += lax.dot_general(dh, we, (((1,), (1,)), ((), ())), preferred_element_type=F32)
    dwe_ref[...] = jnp.dot(nt[...], dh, preferred_element_type=F32).astype(BF)
    dwr_ref[...] = jnp.dot(act.T, up, preferred_element_type=F32).astype(BF)
    dbe_ref[...] = jnp.sum(dh.astype(F32), axis=0, keepdims=True)


def ffn(n, up, we, wr, be, chunk):
    rows, d = n.shape
    ff = we.shape[1]
    whole = pl.BlockSpec((rows, d), lambda i: (0, 0))
    return pl.pallas_call(
        ffn_kernel,
        grid=(ff // chunk,),
        in_specs=[
            whole,
            whole,
            pl.BlockSpec((d, chunk), lambda i: (0, i)),
            pl.BlockSpec((chunk, d), lambda i: (i, 0)),
            pl.BlockSpec((1, chunk), lambda i: (0, i)),
        ],
        out_specs=[
            whole,
            whole,
            pl.BlockSpec((d, chunk), lambda i: (0, i)),
            pl.BlockSpec((chunk, d), lambda i: (i, 0)),
            pl.BlockSpec((1, chunk), lambda i: (0, i)),
        ],
        out_shape=[
            jax.ShapeDtypeStruct((rows, d), F32),
            jax.ShapeDtypeStruct((rows, d), F32),
            jax.ShapeDtypeStruct((d, ff), BF),
            jax.ShapeDtypeStruct((ff, d), BF),
            jax.ShapeDtypeStruct((1, ff), F32),
        ],
        scratch_shapes=[pltpu.VMEM((d, rows), BF)],
        compiler_params=params(1),
        cost_estimate=cost(12 * rows * d * ff, 8 * d * ff + rows * d * 12, 2 * rows * ff),
        name="ffn",
    )(n, up, we, wr, be)


def layer_norm(input_rows, norm_gain, norm_shift):
    centre = jnp.mean(input_rows, axis=-1, keepdims=True)
    centered = input_rows - centre
    spread = jnp.mean(centered * centered, axis=-1, keepdims=True)
    return centered * lax.rsqrt(spread + EPS) * norm_gain + norm_shift


def mul(rows, matrix):
    return jnp.dot(rows, matrix, preferred_element_type=F32)


def mul_back(grad, matrix):
    return lax.dot_general(grad, matrix, (((1,), (1,)), ((), ())), preferred_element_type=F32)


def grad_of(rows, grad):
    return lax.dot_general(
        rows, grad, (((0,), (0,)), ((), ())), preferred_element_type=F32
    ).astype(BF)


def col_sum(grad):
    return jnp.sum(grad.astype(F32), axis=0)


def gather(x, axes):
    return lax.all_gather(x, axes, axis=0, tiled=True)


def scatter(x, axes):
    return lax.psum_scatter(x, axes, scatter_dimension=0, tiled=True)


CTX = ("g", "m")
ALL = ("g", "m", "fsdp")


def body(
    tokens, encoder_states, lengths, cotangent,
    first_gain, first_shift, query_weight, query_bias, key_weight, value_weight, value_bias,
    self_out_weight, self_out_bias, second_gain, second_shift,
    cross_query_weight, cross_query_bias, cross_key_weight, cross_value_weight, cross_value_bias,
    cross_out_weight, cross_out_bias, third_gain, third_shift,
    expand_weight, expand_bias, reduce_weight, reduce_bias,
):
    groups, members, fs = lax.axis_size("g"), lax.axis_size("m"), lax.axis_size("fsdp")
    gi, mi, fi = lax.axis_index("g"), lax.axis_index("m"), lax.axis_index("fsdp")
    ctx = groups * members
    me = gi * members + mi
    tokens, encoder, cotangent = tokens[0], encoder_states[0], cotangent[0]
    local, d = tokens.shape
    total = local * ctx
    shard = d // fs
    ff = expand_weight.shape[1]
    hg = HEADS // groups
    width = hg * HEAD_DIM
    piece = local // members
    frames = encoder.shape[0]
    kt = 512
    padded = -(-frames // kt) * kt
    length = lengths[0]

    vectors = [
        first_gain, first_shift, query_bias, value_bias, self_out_bias, second_gain, second_shift,
        cross_query_bias, cross_value_bias, cross_out_bias, third_gain, third_shift, reduce_bias,
    ]
    ratio = ff // d
    columns = jnp.concatenate(
        [jnp.stack(vectors, axis=1), expand_bias.reshape(shard, ratio)], axis=1
    )
    columns = jnp.pad(columns, ((0, 0), (0, 128 - columns.shape[1])))
    mine = lambda w: lax.dynamic_slice_in_dim(w, gi * width, width, 1)
    first = gather(
        jnp.concatenate([mine(query_weight), mine(key_weight), mine(value_weight), columns], axis=1),
        "fsdp",
    )
    all_tokens = gather(tokens, CTX)
    second = gather(
        jnp.concatenate(
            [self_out_weight, cross_query_weight, cross_key_weight, cross_value_weight, cross_out_weight],
            axis=1,
        ),
        "fsdp",
    )
    so_mat, cq_mat, ck_mat, cv_mat, co_mat = [second[:, i * d : (i + 1) * d] for i in range(5)]
    expand_mat = gather(expand_weight, "fsdp")
    reduce_mat = gather(reduce_weight, "fsdp")
    by_group = lambda w: w.reshape(shard, groups, width)
    qkv_mat = gather(
        jnp.stack([by_group(query_weight), by_group(key_weight), by_group(value_weight)], axis=2).reshape(
            shard, 3 * d
        ),
        "fsdp",
    )
    table = first[:, 3 * width :].astype(F32).T
    (
        gain_one, shift_one, query_add, value_add, so_add, gain_two, shift_two,
        cq_add, cv_add, co_add, gain_three, shift_three, reduce_add,
    ) = [table[i] for i in range(len(vectors))]
    expand_add = first[:, 3 * width + len(vectors) : 3 * width + len(vectors) + ratio].astype(F32).reshape(1, ff)

    own_part = lambda v: lax.dynamic_slice_in_dim(v, gi * width, width, 0)
    qkv_add = jnp.concatenate([own_part(query_add), jnp.zeros((width,), F32), own_part(value_add)])
    normed_all, q, k, v = ln_qkv(
        all_tokens, first[:, : 3 * width], qkv_add[None], gain_one[None], shift_one[None], min(512, total)
    )
    info = jnp.stack([length, mi.astype(jnp.int32)])
    q_index = lambda i, s: i * members + (s[1] + i) % members
    rows_of = lambda i, s: q_index(i, s) * piece
    mixed32, mixed_own, lse = flash_fwd(
        q, k, v, info, hg, piece, kt, True, ctx, q_index, rows_of, "self_fwd"
    )

    def exchange(x):
        return lax.all_to_all(x, CTX, 0, 0, tiled=True)

    def to_rows(x, cols):
        x = x.reshape(groups, members, piece, cols)
        x = lax.dynamic_slice_in_dim(jnp.concatenate([x, x], axis=1), (-me) % members, members, 1)
        return x.transpose(1, 2, 0, 3).reshape(local, groups * cols)

    def to_heads(x):
        x = x.reshape(members, piece, groups, width)
        x = lax.dynamic_slice_in_dim(jnp.concatenate([x, x], axis=0), me % members, members, 0)
        return x.transpose(2, 0, 1, 3).reshape(ctx * piece, width)

    mixed = to_rows(exchange(mixed_own), width)

    residual = tokens.astype(F32)
    after_self = residual + mul(mixed, so_mat) + so_add
    normed_two, norm_back_two = jax.vjp(layer_norm, after_self, gain_two, shift_two)
    normed_two = normed_two.astype(BF)
    cross_query = (mul(normed_two, cq_mat) + cq_add).astype(BF)
    enc = jnp.pad(encoder, ((0, padded - frames), (0, 0)))
    cross_keys = mul(enc, ck_mat).astype(BF)
    cross_values = (mul(enc, cv_mat) + cv_add).astype(BF)
    cross_info = jnp.array([frames, 0], jnp.int32)
    cqt = min(256, local)
    plain = lambda i, s: i
    zero = lambda i, s: 0
    chg = 4
    cross32, cross_rows, cross_lse = flash_fwd(
        cross_query, cross_keys, cross_values, cross_info, chg, cqt, kt, False, local // cqt, plain, zero,
        "cross_fwd",
    )
    after_cross = after_self + mul(cross_rows, co_mat) + co_add
    normed_three, norm_back_three = jax.vjp(layer_norm, after_cross, gain_three, shift_three)
    normed_three = normed_three.astype(BF)

    position = me * local + jnp.arange(local, dtype=jnp.int32)
    valid = (position < length).astype(F32)[:, None]
    up = cotangent.astype(F32) * valid
    reduce_up = up.astype(BF)
    ff_out, ff_back, grad_expand, grad_reduce, grad_expand_add = ffn(
        normed_three, reduce_up, expand_mat, reduce_mat, expand_add, 512
    )
    layer_out = (after_cross + ff_out + reduce_add) * valid
    expand_shard = lax.psum(scatter(grad_expand, "fsdp"), CTX)
    reduce_shard = lax.psum(scatter(grad_reduce, "fsdp"), CTX)
    part, grad_gain_three, grad_shift_three = norm_back_three(ff_back)
    up = up + part

    co_up = up.astype(BF)
    cross_dout = mul_back(co_up, co_mat).astype(BF)
    cq_up, ck_part, cv_part = flash_bwd(
        cross_query, cross_dout, cross32, cross_lse, cross_keys, cross_values, cross_info, chg, cqt, kt,
        False, local // cqt, plain, zero, "cross_bwd",
    )
    enc_up = scatter(jnp.concatenate([ck_part, cv_part], axis=1), CTX)
    enc_rows_count = padded // ctx
    enc_rows = lax.dynamic_slice_in_dim(enc, me * enc_rows_count, enc_rows_count, 0)
    enc_grad_rows = mul_back(enc_up[:, :d], ck_mat) + mul_back(enc_up[:, d:], cv_mat)
    encoder_grads = gather(enc_grad_rows.astype(BF), CTX)[:frames].astype(F32)
    grad_ckv = grad_of(enc_rows, enc_up)
    part, grad_gain_two, grad_shift_two = norm_back_two(mul_back(cq_up, cq_mat))
    up = up + part
    so_up = up.astype(BF)

    self_dout = mul_back(so_up, so_mat).astype(BF)
    dout_own = exchange(to_heads(self_dout))
    grad_mid = jnp.concatenate(
        [grad_of(mixed, so_up), grad_of(normed_two, cq_up), grad_of(cross_rows, co_up)], axis=1
    )
    q_up, k_part, v_part = flash_bwd(
        q, dout_own, mixed32, lse, k, v, info, hg, piece, kt, True, ctx, q_index, rows_of, "self_bwd"
    )
    mid_shard = lax.psum(scatter(grad_mid, "fsdp"), CTX)
    ckv_shard = lax.psum(scatter(grad_ckv, "fsdp"), CTX)

    def pick(x, member):
        x = x.reshape(ctx, members, piece, x.shape[-1])
        which = ((member + jnp.arange(ctx)) % members)[:, None, None]
        out = x[:, 0]
        for c in range(1, members):
            out = jnp.where(which == c, x[:, c], out)
        return out.reshape(ctx * piece, x.shape[-1])

    kv_part = jnp.concatenate([k_part, v_part], axis=1)
    kv_up = pick(kv_part, mi).astype(F32)
    for hop in range(1, members):
        kv_up = kv_up + lax.ppermute(
            pick(kv_part, mi + hop), "m", [(i, (i + hop) % members) for i in range(members)]
        ).astype(F32)
    qkv_up = jnp.concatenate([q_up, kv_up.astype(BF)], axis=1)
    qkv_rows = to_rows(exchange(qkv_up), 3 * width)
    grad_qkv = grad_of(pick(normed_all, mi), qkv_up)
    qkv_shard = gather(lax.psum(scatter(grad_qkv, "fsdp"), "m"), "g").reshape(groups, shard, 3, width)
    query_shard, key_shard, value_shard = [
        qkv_shard[:, :, i].transpose(1, 0, 2).reshape(shard, d) for i in range(3)
    ]
    _, norm_back_one = jax.vjp(layer_norm, residual, gain_one, shift_one)
    part, grad_gain_one, grad_shift_one = norm_back_one(mul_back(qkv_rows, qkv_mat))
    token_grads = up + part

    def place(x):
        return lax.dynamic_update_slice_in_dim(jnp.zeros((d,), F32), x, gi * width, 0)

    sums = jnp.stack(
        [
            grad_gain_one, grad_shift_one,
            place(col_sum(q_up)), place(col_sum(qkv_up[:, 2 * width :])),
            col_sum(so_up), grad_gain_two, grad_shift_two,
            col_sum(cq_up), col_sum(enc_up[:, d:]), col_sum(co_up),
            grad_gain_three, grad_shift_three, col_sum(reduce_up),
        ]
    )
    sums = jnp.concatenate([sums, grad_expand_add.reshape(ratio, d)], axis=0)
    sums = lax.psum(sums, ALL)
    vec = lax.dynamic_slice_in_dim(sums[: len(vectors)], fi * shard, shard, 1)
    expand_vec = lax.dynamic_slice_in_dim(sums[len(vectors) :].reshape(ff), fi * (ff // fs), ff // fs, 0)
    vec = [vec[i] for i in range(len(vectors))]
    f32 = lambda x: x.astype(F32)
    mid = [f32(mid_shard[:, i * d : (i + 1) * d]) for i in range(3)]
    return (
        layer_out[None], token_grads[None], encoder_grads[None],
        vec[0], vec[1], f32(query_shard), vec[2], f32(key_shard), f32(value_shard), vec[3],
        mid[0], vec[4], vec[5], vec[6], mid[1], vec[7],
        f32(ckv_shard[:, :d]), f32(ckv_shard[:, d:]), vec[8], mid[2], vec[9],
        vec[10], vec[11], f32(expand_shard), expand_vec, f32(reduce_shard), vec[12],
    )


def solution(mesh):
    ctx, fs = mesh.shape["ctx"], mesh.shape["fsdp"]
    groups = math.gcd(HEADS, ctx // 2)
    split = Mesh(mesh.devices.reshape(groups, ctx // groups, fs), ("g", "m", "fsdp"))
    rows, slot, vec, mat = P("fsdp", CTX, None), P("fsdp", None, None), P("fsdp"), P("fsdp", None)
    weights = (
        vec, vec, mat, vec, mat, mat, vec, mat, vec, vec, vec, mat, vec, mat, mat, vec, mat, vec,
        vec, vec, mat, vec, mat, vec,
    )
    return jax.shard_map(
        body,
        mesh=split,
        in_specs=(rows, slot, vec, rows) + weights,
        out_specs=(rows, rows, slot) + weights,
        check_vma=False,
    )
```

```python
import functools
import math

import jax
import jax.numpy as jnp
from jax import lax
from jax.experimental import pallas as pl
from jax.experimental.pallas import tpu as pltpu
from jax.sharding import Mesh
from jax.sharding import PartitionSpec as P

HEADS = 12
HEAD_DIM = 64
SCALE = HEAD_DIM ** (-0.5)
EPS = 1e-05
MASKED = -1e30
BF = jnp.bfloat16
F32 = jnp.float32


def cost(flops, nbytes, exps=0):
    return pl.CostEstimate(flops=int(flops), bytes_accessed=int(nbytes), transcendentals=int(exps))


def params(axes):
    return pltpu.CompilerParams(
        dimension_semantics=("arbitrary",) * axes, vmem_limit_bytes=60 * 1024 * 1024
    )


def masked_heads(flat, hg):
    zero = jnp.zeros((HEAD_DIM, flat.shape[1]), flat.dtype)
    out = []
    for h in range(hg):
        rows = [zero] * hg
        rows[h] = flat[h * HEAD_DIM : (h + 1) * HEAD_DIM]
        out.append(jnp.concatenate(rows, axis=0))
    return out


def tile_mask(block_pos, tile_start, shape, length, causal):
    key = tile_start + lax.broadcasted_iota(jnp.int32, shape, 0)
    inside = key < length
    if causal:
        query = block_pos + lax.broadcasted_iota(jnp.int32, shape, 1)
        inside = inside & (key <= query)
    return inside


def tile_bounds(base, qt, kt, length, causal, total):
    if causal:
        full = jnp.minimum(base, length) // kt
        end = (jnp.minimum(base + qt, length) + kt - 1) // kt
        return full, end
    return length // kt, (length + kt - 1) // kt


def fwd_kernel(hg, qt, kt, causal, rows_of, info, q_ref, k_ref, v_ref, o_ref, ob_ref, lse_ref,
               vt, qm, acc, mx, sm):
    block = pl.program_id(1)
    total = k_ref.shape[0]
    width = hg * HEAD_DIM

    @pl.when(block == 0)
    def _():
        vt[...] = v_ref[...].T

    flat = (q_ref[...] * BF(SCALE)).T
    for h, piece in enumerate(masked_heads(flat, hg)):
        qm[h] = piece
    acc[...] = jnp.zeros_like(acc)
    sm[...] = jnp.zeros_like(sm)
    mx[...] = jnp.full_like(mx, MASKED)
    base = rows_of(block, info)
    length = info[0]

    def step(j, masked):
        start = pl.multiple_of(j * kt, kt)
        keys = k_ref[pl.ds(start, kt), :]
        if masked:
            allowed = tile_mask(base, start, (kt, qt), length, causal)
        scores, tops = [], []
        for h in range(hg):
            s = jnp.dot(keys, qm[h], preferred_element_type=F32)
            if masked:
                s = jnp.where(allowed, s, MASKED)
            scores.append(s)
            tops.append(jnp.max(s, axis=0, keepdims=True))
        for h in range(hg):
            old = mx[h : h + 1, :]
            new = jnp.maximum(old, tops[h])
            p = jnp.exp(scores[h] - new)
            fix = jnp.exp(old - new)
            mx[h : h + 1, :] = new
            sm[h : h + 1, :] = sm[h : h + 1, :] * fix + jnp.sum(p, axis=0, keepdims=True)
            here = slice(h * HEAD_DIM, (h + 1) * HEAD_DIM)
            acc[here, :] = acc[here, :] * fix + jnp.dot(
                vt[here, pl.ds(start, kt)], p.astype(BF), preferred_element_type=F32
            )

    if causal:
        full, end = tile_bounds(base, qt, kt, length, causal, total)

        @pl.loop(0, full)
        def _(j):
            step(j, False)

        @pl.loop(full, end)
        def _(j):
            step(j, True)
    else:
        tiles = total // kt
        for j in range(tiles):
            step(j, j == tiles - 1)

    for h in range(hg):
        here = slice(h * HEAD_DIM, (h + 1) * HEAD_DIM)
        acc[here, :] = acc[here, :] / sm[h : h + 1, :]
    out = acc[...].T
    o_ref[...] = out
    ob_ref[...] = out.astype(BF)
    lse_ref[0, 0] = mx[:hg, :] + jnp.log(sm[:hg, :])


def bwd_kernel(hg, qt, kt, causal, rows_of, info, q_ref, do_ref, o_ref, lse_ref, k_ref, v_ref,
               dq_ref, dk_ref, dv_ref, kt_ref, qm, dm, qs, ds_, dk, dv, dqt, dl):
    block = pl.program_id(1)
    total = k_ref.shape[0]

    @pl.when(block == 0)
    def _():
        kt_ref[...] = k_ref[...].T
        dk[...] = jnp.zeros_like(dk)
        dv[...] = jnp.zeros_like(dv)

    q = q_ref[...] * BF(SCALE)
    do = do_ref[...]
    qflat = q.T
    dflat = do.T
    prod = (do.astype(F32) * o_ref[...]).T
    lane = lax.broadcasted_iota(jnp.int32, (qt, hg * HEAD_DIM), 1) // HEAD_DIM
    qpieces = masked_heads(qflat, hg)
    dpieces = masked_heads(dflat, hg)
    for h in range(hg):
        qm[h] = qpieces[h]
        dm[h] = dpieces[h]
        keep = lane == h
        qs[h * qt : (h + 1) * qt, :] = jnp.where(keep, q, jnp.zeros_like(q))
        ds_[h * qt : (h + 1) * qt, :] = jnp.where(keep, do, jnp.zeros_like(do))
        dl[h : h + 1, :] = jnp.sum(prod[h * HEAD_DIM : (h + 1) * HEAD_DIM], axis=0, keepdims=True)
    dqt[...] = jnp.zeros_like(dqt)
    base = rows_of(block, info)
    length = info[0]

    def step(j, masked):
        start = pl.multiple_of(j * kt, kt)
        keys = k_ref[pl.ds(start, kt), :]
        values = v_ref[pl.ds(start, kt), :]
        if masked:
            allowed = tile_mask(base, start, (kt, qt), length, causal)
        ps, gs = [], []
        for h in range(hg):
            s = jnp.dot(keys, qm[h], preferred_element_type=F32)
            p = jnp.exp(s - lse_ref[0, 0, h : h + 1, :])
            if masked:
                p = jnp.where(allowed, p, 0.0)
            dp = jnp.dot(values, dm[h], preferred_element_type=F32)
            g = (p * (dp - dl[h : h + 1, :])).astype(BF)
            ps.append(p.astype(BF))
            gs.append(g)
            here = slice(h * HEAD_DIM, (h + 1) * HEAD_DIM)
            dqt[here, :] += jnp.dot(kt_ref[here, pl.ds(start, kt)], g, preferred_element_type=F32)
        where = pl.ds(start, kt)
        dv[where, :] += jnp.dot(
            jnp.concatenate(ps, axis=1), ds_[...], preferred_element_type=F32
        )
        dk[where, :] += jnp.dot(
            jnp.concatenate(gs, axis=1), qs[...], preferred_element_type=F32
        )

    if causal:
        full, end = tile_bounds(base, qt, kt, length, causal, total)

        @pl.loop(0, full)
        def _(j):
            step(j, False)

        @pl.loop(full, end)
        def _(j):
            step(j, True)
    else:
        tiles = total // kt
        for j in range(tiles):
            step(j, j == tiles - 1)

    dq_ref[...] = (dqt[...] * SCALE).T.astype(BF)

    @pl.when(block == pl.num_programs(1) - 1)
    def _():
        dk_ref[...] = dk[...].astype(BF)
        dv_ref[...] = dv[...].astype(BF)


def flash_fwd(q, k, v, info, hg, qt, kt, causal, blocks, q_index, rows_of, name):
    total, all_width = k.shape
    width = hg * HEAD_DIM
    groups = all_width // width
    rows = blocks * qt
    pairs = rows * total * HEADS * (1 if not causal else 0.5) * groups * hg / HEADS
    return pl.pallas_call(
        functools.partial(fwd_kernel, hg, qt, kt, causal, rows_of),
        grid_spec=pltpu.PrefetchScalarGridSpec(
            num_scalar_prefetch=1,
            grid=(groups, blocks),
            in_specs=[
                pl.BlockSpec((qt, width), lambda g, i, s: (q_index(i, s), g)),
                pl.BlockSpec((total, width), lambda g, i, s: (0, g)),
                pl.BlockSpec((total, width), lambda g, i, s: (0, g)),
            ],
            out_specs=[
                pl.BlockSpec((qt, width), lambda g, i, s: (i, g)),
                pl.BlockSpec((qt, width), lambda g, i, s: (i, g)),
                pl.BlockSpec((1, 1, hg, qt), lambda g, i, s: (g, i, 0, 0)),
            ],
            scratch_shapes=[
                pltpu.VMEM((width, total), BF),
                pltpu.VMEM((hg, width, qt), BF),
                pltpu.VMEM((width, qt), F32),
                pltpu.VMEM((8, qt), F32),
                pltpu.VMEM((8, qt), F32),
            ],
        ),
        out_shape=[
            jax.ShapeDtypeStruct((rows, all_width), F32),
            jax.ShapeDtypeStruct((rows, all_width), BF),
            jax.ShapeDtypeStruct((groups, blocks, hg, qt), F32),
        ],
        compiler_params=params(2),
        cost_estimate=cost(pairs * 4 * 256, rows * all_width * 8 + total * all_width * 4, pairs),
        name=name,
    )(info, q, k, v)


def flash_bwd(q, do, o, lse, k, v, info, hg, qt, kt, causal, blocks, q_index, rows_of, name):
    total, all_width = k.shape
    width = hg * HEAD_DIM
    groups = all_width // width
    rows = blocks * qt
    pairs = rows * total * HEADS * (1 if not causal else 0.5) * groups * hg / HEADS
    return pl.pallas_call(
        functools.partial(bwd_kernel, hg, qt, kt, causal, rows_of),
        grid_spec=pltpu.PrefetchScalarGridSpec(
            num_scalar_prefetch=1,
            grid=(groups, blocks),
            in_specs=[
                pl.BlockSpec((qt, width), lambda g, i, s: (q_index(i, s), g)),
                pl.BlockSpec((qt, width), lambda g, i, s: (i, g)),
                pl.BlockSpec((qt, width), lambda g, i, s: (i, g)),
                pl.BlockSpec((1, 1, hg, qt), lambda g, i, s: (g, i, 0, 0)),
                pl.BlockSpec((total, width), lambda g, i, s: (0, g)),
                pl.BlockSpec((total, width), lambda g, i, s: (0, g)),
            ],
            out_specs=[
                pl.BlockSpec((qt, width), lambda g, i, s: (i, g)),
                pl.BlockSpec((total, width), lambda g, i, s: (0, g)),
                pl.BlockSpec((total, width), lambda g, i, s: (0, g)),
            ],
            scratch_shapes=[
                pltpu.VMEM((width, total), BF),
                pltpu.VMEM((hg, width, qt), BF),
                pltpu.VMEM((hg, width, qt), BF),
                pltpu.VMEM((hg * qt, width), BF),
                pltpu.VMEM((hg * qt, width), BF),
                pltpu.VMEM((total, width), F32),
                pltpu.VMEM((total, width), F32),
                pltpu.VMEM((width, qt), F32),
                pltpu.VMEM((8, qt), F32),
            ],
        ),
        out_shape=[
            jax.ShapeDtypeStruct((rows, all_width), BF),
            jax.ShapeDtypeStruct((total, all_width), BF),
            jax.ShapeDtypeStruct((total, all_width), BF),
        ],
        compiler_params=params(2),
        cost_estimate=cost(pairs * 10 * 256, rows * all_width * 10 + total * all_width * 8, pairs),
        name=name,
    )(info, q, do, o, lse, k, v)


def ln_qkv_kernel(x_ref, w_ref, add_ref, gain_ref, shift_ref, n_ref, q_ref, k_ref, v_ref):
    x = x_ref[...].astype(F32)
    centre = jnp.mean(x, axis=-1, keepdims=True)
    x = x - centre
    spread = jnp.mean(x * x, axis=-1, keepdims=True)
    n = (x * lax.rsqrt(spread + EPS) * gain_ref[...] + shift_ref[...]).astype(BF)
    n_ref[...] = n
    width = q_ref.shape[1]
    y = jnp.dot(n, w_ref[...], preferred_element_type=F32) + add_ref[...]
    y = y.astype(BF)
    q_ref[...] = y[:, :width]
    k_ref[...] = y[:, width : 2 * width]
    v_ref[...] = y[:, 2 * width :]


def ln_qkv(x, w, add, gain, shift, rows):
    total, d = x.shape
    width = w.shape[1] // 3
    whole = lambda a: pl.BlockSpec(a.shape, lambda i: (0, 0))
    return pl.pallas_call(
        ln_qkv_kernel,
        grid=(total // rows,),
        in_specs=[pl.BlockSpec((rows, d), lambda i: (i, 0)), whole(w), whole(add), whole(gain), whole(shift)],
        out_specs=[pl.BlockSpec((rows, d), lambda i: (i, 0))]
        + [pl.BlockSpec((rows, width), lambda i: (i, 0))] * 3,
        out_shape=[jax.ShapeDtypeStruct((total, d), BF)]
        + [jax.ShapeDtypeStruct((total, width), BF)] * 3,
        compiler_params=params(1),
        cost_estimate=cost(2 * total * d * 3 * width, total * d * 4 + total * width * 6),
        name="ln_qkv",
    )(x, w, add, gain, shift)


def ffn_kernel(n_ref, up_ref, we_ref, wr_ref, be_ref, out_ref, dn_ref, dwe_ref, dwr_ref, dbe_ref, nt):
    step = pl.program_id(0)

    @pl.when(step == 0)
    def _():
        nt[...] = n_ref[...].T
        out_ref[...] = jnp.zeros_like(out_ref)
        dn_ref[...] = jnp.zeros_like(dn_ref)

    we = we_ref[...]
    wr = wr_ref[...]
    up = up_ref[...]
    h = jnp.dot(n_ref[...], we, preferred_element_type=F32) + be_ref[...]
    half = 0.5 + 0.5 * lax.erf(h * (2.0**-0.5))
    act = (h * half).astype(BF)
    slope = half + h * jnp.exp(-0.5 * h * h) * ((2.0 * math.pi) ** -0.5)
    out_ref[...] += jnp.dot(act, wr, preferred_element_type=F32)
    da = lax.dot_general(up, wr, (((1,), (1,)), ((), ())), preferred_element_type=F32)
    dh32 = da * slope
    dh = dh32.astype(BF)
    dn_ref[...] += lax.dot_general(dh, we, (((1,), (1,)), ((), ())), preferred_element_type=F32)
    dwe_ref[...] = jnp.dot(nt[...], dh, preferred_element_type=F32).astype(BF)
    dwr_ref[...] = jnp.dot(act.T, up, preferred_element_type=F32).astype(BF)
    dbe_ref[...] = jnp.sum(dh.astype(F32), axis=0, keepdims=True)


def ffn(n, up, we, wr, be, chunk):
    rows, d = n.shape
    ff = we.shape[1]
    whole = pl.BlockSpec((rows, d), lambda i: (0, 0))
    return pl.pallas_call(
        ffn_kernel,
        grid=(ff // chunk,),
        in_specs=[
            whole,
            whole,
            pl.BlockSpec((d, chunk), lambda i: (0, i)),
            pl.BlockSpec((chunk, d), lambda i: (i, 0)),
            pl.BlockSpec((1, chunk), lambda i: (0, i)),
        ],
        out_specs=[
            whole,
            whole,
            pl.BlockSpec((d, chunk), lambda i: (0, i)),
            pl.BlockSpec((chunk, d), lambda i: (i, 0)),
            pl.BlockSpec((1, chunk), lambda i: (0, i)),
        ],
        out_shape=[
            jax.ShapeDtypeStruct((rows, d), F32),
            jax.ShapeDtypeStruct((rows, d), F32),
            jax.ShapeDtypeStruct((d, ff), BF),
            jax.ShapeDtypeStruct((ff, d), BF),
            jax.ShapeDtypeStruct((1, ff), F32),
        ],
        scratch_shapes=[pltpu.VMEM((d, rows), BF)],
        compiler_params=params(1),
        cost_estimate=cost(12 * rows * d * ff, 8 * d * ff + rows * d * 12, 2 * rows * ff),
        name="ffn",
    )(n, up, we, wr, be)


def layer_norm(input_rows, norm_gain, norm_shift):
    centre = jnp.mean(input_rows, axis=-1, keepdims=True)
    centered = input_rows - centre
    spread = jnp.mean(centered * centered, axis=-1, keepdims=True)
    return centered * lax.rsqrt(spread + EPS) * norm_gain + norm_shift


def mul(rows, matrix):
    return jnp.dot(rows, matrix, preferred_element_type=F32)


def mul_back(grad, matrix):
    return lax.dot_general(grad, matrix, (((1,), (1,)), ((), ())), preferred_element_type=F32)


def grad_of(rows, grad):
    return lax.dot_general(
        rows, grad, (((0,), (0,)), ((), ())), preferred_element_type=F32
    ).astype(BF)


def col_sum(grad):
    return jnp.sum(grad.astype(F32), axis=0)


def gather(x, axes):
    return lax.all_gather(x, axes, axis=0, tiled=True)


def scatter(x, axes):
    return lax.psum_scatter(x, axes, scatter_dimension=0, tiled=True)


CHIPS = ("g", "p")
CTX = ("g", "p", "c")
ALL = ("g", "p", "c", "fsdp")
SWAP = [(0, 1), (1, 0)]


def body(
    tokens, encoder_states, lengths, cotangent,
    first_gain, first_shift, query_weight, query_bias, key_weight, value_weight, value_bias,
    self_out_weight, self_out_bias, second_gain, second_shift,
    cross_query_weight, cross_query_bias, cross_key_weight, cross_value_weight, cross_value_bias,
    cross_out_weight, cross_out_bias, third_gain, third_shift,
    expand_weight, expand_bias, reduce_weight, reduce_bias,
):
    groups, fs = lax.axis_size("g"), lax.axis_size("fsdp")
    members = lax.axis_size(("p", "c"))
    gi, mi, fi = lax.axis_index("g"), lax.axis_index(("p", "c")), lax.axis_index("fsdp")
    core = lax.axis_index("c")
    ctx = groups * members
    me = gi * members + mi
    tokens, encoder, cotangent = tokens[0], encoder_states[0], cotangent[0]
    local, d = tokens.shape
    total = local * ctx
    shard = d // fs
    ff = expand_weight.shape[1]
    hg = HEADS // groups
    width = hg * HEAD_DIM
    piece = local // members
    frames = encoder.shape[0]
    kt = 512
    padded = -(-frames // kt) * kt
    length = lengths[0]

    vectors = [
        first_gain, first_shift, query_bias, value_bias, self_out_bias, second_gain, second_shift,
        cross_query_bias, cross_value_bias, cross_out_bias, third_gain, third_shift, reduce_bias,
    ]
    ratio = ff // d
    columns = jnp.concatenate(
        [jnp.stack(vectors, axis=1), expand_bias.reshape(shard, ratio)], axis=1
    )
    columns = jnp.pad(columns, ((0, 0), (0, 128 - columns.shape[1])))
    mine = lambda w: lax.dynamic_slice_in_dim(w, gi * width, width, 1)
    first = gather(
        jnp.concatenate([mine(query_weight), mine(key_weight), mine(value_weight), columns], axis=1),
        "fsdp",
    )
    all_tokens = gather(tokens, CTX)
    second = gather(
        jnp.concatenate(
            [self_out_weight, cross_query_weight, cross_key_weight, cross_value_weight, cross_out_weight],
            axis=1,
        ),
        "fsdp",
    )
    so_mat, cq_mat, ck_mat, cv_mat, co_mat = [second[:, i * d : (i + 1) * d] for i in range(5)]
    expand_mat = gather(expand_weight, "fsdp")
    reduce_mat = gather(reduce_weight, "fsdp")
    by_group = lambda w: w.reshape(shard, groups, width)
    qkv_mat = gather(
        jnp.stack([by_group(query_weight), by_group(key_weight), by_group(value_weight)], axis=2).reshape(
            shard, 3 * d
        ),
        "fsdp",
    )
    table = first[:, 3 * width :].astype(F32).T
    (
        gain_one, shift_one, query_add, value_add, so_add, gain_two, shift_two,
        cq_add, cv_add, co_add, gain_three, shift_three, reduce_add,
    ) = [table[i] for i in range(len(vectors))]
    expand_add = first[:, 3 * width + len(vectors) : 3 * width + len(vectors) + ratio].astype(F32).reshape(1, ff)

    own_part = lambda v: lax.dynamic_slice_in_dim(v, gi * width, width, 0)
    qkv_add = jnp.concatenate([own_part(query_add), jnp.zeros((width,), F32), own_part(value_add)])
    normed_all, q, k, v = ln_qkv(
        all_tokens, first[:, : 3 * width], qkv_add[None], gain_one[None], shift_one[None], min(512, total)
    )
    info = jnp.stack([length, mi.astype(jnp.int32)])
    q_index = lambda i, s: i * members + (s[1] + i) % members
    rows_of = lambda i, s: q_index(i, s) * piece
    mixed32, mixed_own, lse = flash_fwd(
        q, k, v, info, hg, piece, kt, True, ctx, q_index, rows_of, "self_fwd"
    )

    def exchange(x):
        return lax.all_to_all(x, CTX, 0, 0, tiled=True)

    def to_rows(x, cols):
        x = x.reshape(groups, members, piece, cols)
        x = lax.dynamic_slice_in_dim(jnp.concatenate([x, x], axis=1), (-me) % members, members, 1)
        return x.transpose(1, 2, 0, 3).reshape(local, groups * cols)

    def to_heads(x):
        x = x.reshape(members, piece, groups, width)
        x = lax.dynamic_slice_in_dim(jnp.concatenate([x, x], axis=0), me % members, members, 0)
        return x.transpose(2, 0, 1, 3).reshape(ctx * piece, width)

    mixed = to_rows(exchange(mixed_own), width)

    def half(x, which):
        return lax.dynamic_slice_in_dim(x, which * (x.shape[1] // 2), x.shape[1] // 2, 1)

    def on_chip(x):
        other = lax.ppermute(half(x, 1 - core), "c", SWAP)
        return (half(x, core).astype(F32) + other.astype(F32)).astype(BF)

    def over_fsdp(x):
        x = lax.all_to_all(x.reshape(fs, x.shape[0] // fs, x.shape[1]), "fsdp", 0, 0)
        return jnp.sum(x.astype(F32), axis=0).astype(BF)

    def whole(x):
        other = lax.ppermute(x, "c", SWAP)
        low, high = jnp.where(core == 0, x, other), jnp.where(core == 0, other, x)
        return jnp.concatenate([low, high], axis=1).astype(F32)

    residual = tokens.astype(F32)
    after_self = residual + mul(mixed, so_mat) + so_add
    normed_two, norm_back_two = jax.vjp(layer_norm, after_self, gain_two, shift_two)
    normed_two = normed_two.astype(BF)
    cross_query = (mul(normed_two, cq_mat) + cq_add).astype(BF)
    enc = jnp.pad(encoder, ((0, padded - frames), (0, 0)))
    cross_keys = mul(enc, ck_mat).astype(BF)
    cross_values = (mul(enc, cv_mat) + cv_add).astype(BF)
    cross_info = jnp.array([frames, 0], jnp.int32)
    cqt = min(256, local)
    plain = lambda i, s: i
    zero = lambda i, s: 0
    chg = 4
    cross32, cross_rows, cross_lse = flash_fwd(
        cross_query, cross_keys, cross_values, cross_info, chg, cqt, kt, False, local // cqt, plain, zero,
        "cross_fwd",
    )
    after_cross = after_self + mul(cross_rows, co_mat) + co_add
    normed_three, norm_back_three = jax.vjp(layer_norm, after_cross, gain_three, shift_three)
    normed_three = normed_three.astype(BF)

    position = me * local + jnp.arange(local, dtype=jnp.int32)
    valid = (position < length).astype(F32)[:, None]
    up = cotangent.astype(F32) * valid
    reduce_up = up.astype(BF)
    ff_out, ff_back, grad_expand, grad_reduce, grad_expand_add = ffn(
        normed_three, reduce_up, expand_mat, reduce_mat, expand_add, 512
    )
    layer_out = (after_cross + ff_out + reduce_add) * valid
    ffn_shards = [over_fsdp(on_chip(grad_expand)), over_fsdp(on_chip(grad_reduce))]
    part, grad_gain_three, grad_shift_three = norm_back_three(ff_back)
    up = up + part

    co_up = up.astype(BF)
    cross_dout = mul_back(co_up, co_mat).astype(BF)
    cross_dout, qkv_mat = lax.optimization_barrier((cross_dout, qkv_mat))
    cq_up, ck_part, cv_part = flash_bwd(
        cross_query, cross_dout, cross32, cross_lse, cross_keys, cross_values, cross_info, chg, cqt, kt,
        False, local // cqt, plain, zero, "cross_bwd",
    )
    cq_up, ffn_shards = lax.optimization_barrier((cq_up, ffn_shards))
    enc_up = scatter(jnp.concatenate([ck_part, cv_part], axis=1), CTX)
    enc_rows_count = padded // ctx
    enc_rows = lax.dynamic_slice_in_dim(enc, me * enc_rows_count, enc_rows_count, 0)
    part, grad_gain_two, grad_shift_two = norm_back_two(mul_back(cq_up, cq_mat))
    up = up + part
    so_up = up.astype(BF)

    self_dout = mul_back(so_up, so_mat).astype(BF)
    grad_mid = on_chip(
        jnp.concatenate(
        [grad_of(mixed, so_up), grad_of(normed_two, cq_up), grad_of(cross_rows, co_up)], axis=1
        )
    )
    dout_own = exchange(to_heads(self_dout))
    dout_own, grad_mid = lax.optimization_barrier((dout_own, grad_mid))
    q_up, k_part, v_part = flash_bwd(
        q, dout_own, mixed32, lse, k, v, info, hg, piece, kt, True, ctx, q_index, rows_of, "self_bwd"
    )
    mid_shard = over_fsdp(grad_mid)
    q_up, mid_shard, enc_up, ffn_shards = lax.optimization_barrier(
        (q_up, mid_shard, enc_up, [lax.psum(x, CHIPS) for x in ffn_shards])
    )
    enc_grad_rows = mul_back(enc_up[:, :d], ck_mat) + mul_back(enc_up[:, d:], cv_mat)
    encoder_grads = gather(enc_grad_rows.astype(BF), CTX)[:frames].astype(F32)
    grad_ckv = grad_of(enc_rows, enc_up)
    ckv_shard = whole(lax.psum(over_fsdp(on_chip(grad_ckv)), CHIPS))
    mid_shard = whole(lax.psum(mid_shard, CHIPS))
    expand_shard, reduce_shard = [whole(x) for x in ffn_shards]

    def pick(x, member):
        x = x.reshape(ctx, members, piece, x.shape[-1])
        which = ((member + jnp.arange(ctx)) % members)[:, None, None]
        out = x[:, 0]
        for c in range(1, members):
            out = jnp.where(which == c, x[:, c], out)
        return out.reshape(ctx * piece, x.shape[-1])

    kv_part = jnp.concatenate([k_part, v_part], axis=1)
    kv_up = pick(kv_part, mi).astype(F32)
    for hop in range(1, members):
        kv_up = kv_up + lax.ppermute(
            pick(kv_part, mi + hop), ("p", "c"), [(i, (i + hop) % members) for i in range(members)]
        ).astype(F32)
    qkv_up = jnp.concatenate([q_up, kv_up.astype(BF)], axis=1)
    qkv_rows = to_rows(exchange(qkv_up), 3 * width)
    grad_qkv = grad_of(pick(normed_all, mi), qkv_up)
    qkv_shard = gather(lax.psum(scatter(grad_qkv, "fsdp"), ("p", "c")), "g").reshape(groups, shard, 3, width)
    query_shard, key_shard, value_shard = [
        qkv_shard[:, :, i].transpose(1, 0, 2).reshape(shard, d) for i in range(3)
    ]
    _, norm_back_one = jax.vjp(layer_norm, residual, gain_one, shift_one)
    part, grad_gain_one, grad_shift_one = norm_back_one(mul_back(qkv_rows, qkv_mat))
    token_grads = up + part

    def place(x):
        return lax.dynamic_update_slice_in_dim(jnp.zeros((d,), F32), x, gi * width, 0)

    sums = jnp.stack(
        [
            grad_gain_one, grad_shift_one,
            place(col_sum(q_up)), place(col_sum(qkv_up[:, 2 * width :])),
            col_sum(so_up), grad_gain_two, grad_shift_two,
            col_sum(cq_up), col_sum(enc_up[:, d:]), col_sum(co_up),
            grad_gain_three, grad_shift_three, col_sum(reduce_up),
        ]
    )
    sums = jnp.concatenate([sums, grad_expand_add.reshape(ratio, d)], axis=0)
    sums = lax.psum(sums, ALL)
    vec = lax.dynamic_slice_in_dim(sums[: len(vectors)], fi * shard, shard, 1)
    expand_vec = lax.dynamic_slice_in_dim(sums[len(vectors) :].reshape(ff), fi * (ff // fs), ff // fs, 0)
    vec = [vec[i] for i in range(len(vectors))]
    f32 = lambda x: x.astype(F32)
    mid = [f32(mid_shard[:, i * d : (i + 1) * d]) for i in range(3)]
    return (
        layer_out[None], token_grads[None], encoder_grads[None],
        vec[0], vec[1], f32(query_shard), vec[2], f32(key_shard), f32(value_shard), vec[3],
        mid[0], vec[4], vec[5], vec[6], mid[1], vec[7],
        f32(ckv_shard[:, :d]), f32(ckv_shard[:, d:]), vec[8], mid[2], vec[9],
        vec[10], vec[11], f32(expand_shard), expand_vec, f32(reduce_shard), vec[12],
    )


def solution(mesh):
    ctx, fs = mesh.shape["ctx"], mesh.shape["fsdp"]
    groups = math.gcd(HEADS, ctx // 2)
    split = Mesh(
        mesh.devices.reshape(groups, ctx // groups // 2, 2, fs), ("g", "p", "c", "fsdp")
    )
    rows, slot, vec, mat = P("fsdp", CTX, None), P("fsdp", None, None), P("fsdp"), P("fsdp", None)
    weights = (
        vec, vec, mat, vec, mat, mat, vec, mat, vec, vec, vec, mat, vec, mat, mat, vec, mat, vec,
        vec, vec, mat, vec, mat, vec,
    )
    return jax.shard_map(
        body,
        mesh=split,
        in_specs=(rows, slot, vec, rows) + weights,
        out_specs=(rows, rows, slot) + weights,
        check_vma=False,
    )
```
